32 devices in a mesh: rows: 8 (over z, y), grp: 4 (over x, core).
Axes of the slice: x: 2, y: 2, z: 4, core: 2. Of those that a mesh axis runs over, the one named last changes fastest.
Arguments:
- mat: float32 [16384, 1024], P(('rows', 'grp'))
- signs: int32 [16384], P(('rows', 'grp')), may hold values from -1 to 1, as said below
- picks: int32 [2048], P(('rows', 'grp')), may hold values from 0 to 16383, as said below
- rhs: float32 [16384, 128], P(('rows', 'grp'))
Outputs:
- tri: float32 [1024, 1024], replicated
- solution: float32 [1024, 128], replicated
- residual: float32 [16384, 128], P(('rows', 'grp'))
The draws below stay inside these ranges and needn't reach their ends.
Inputs may be any that keep to these rules, and one draw needn't show every extreme that they name: `signs`: every entry is -1 or 1. `picks`: the entries k * 64 to (k + 1) * 64 - 1 are distinct row indices in k * 512 to (k + 1) * 512 - 1.
All inputs are finite; a program needn't handle non-finite values.
Results may differ from the reference program's by a relative error of at most 0.000088.
Values sent between devices are 32-bit elements; how exact they have to be, the bound alone decides.
A program may use at most 64 MiB of HBM per device.

```python
import math
import jax
import jax.numpy as jnp
from jax import lax

N = 1024
L = 512
SAMP_DEV = 64
K = 128
M = 16384


def row_profile(key, rough_low, rough_high):
    ramp = 1.0 + 2.0 * jnp.arange(M, dtype=jnp.float32) / max(M - 1, 1)
    rough = jnp.exp(jax.random.uniform(key, (M,), jnp.float32, math.log(rough_low), math.log(rough_high)))
    return ramp * rough


def draw_mat(key, part):
    entries = jax.random.normal(jax.random.fold_in(key, 1), (M, N), jnp.float32)
    col_scale = jnp.exp(jax.random.uniform(jax.random.fold_in(key, 2), (N,), jnp.float32, 0.0, math.log(10.0)))
    row_scale = row_profile(jax.random.fold_in(key, 3), 0.7, 1.4)
    return (entries * col_scale[None, :] * row_scale[:, None] / math.sqrt(M)).astype(jnp.float32)


def draw_rhs(key, part):
    entries = jax.random.normal(jax.random.fold_in(key, 21), (M, K), jnp.float32)
    row_scale = row_profile(jax.random.fold_in(key, 23), 0.7, 1.4)
    return (entries * row_scale[:, None]).astype(jnp.float32)


def draw_signs(key, part):
    coins = jax.random.randint(jax.random.fold_in(key, 31), (M,), 0, 2)
    return (2 * coins - 1).astype(jnp.int32)


def draw_picks(key, part):
    block_count = M // L
    block_keys = jax.random.split(jax.random.fold_in(key, 41), block_count)
    block_ids = jnp.arange(block_count, dtype=jnp.int32)
    free_value = jax.random.randint(jax.random.fold_in(key, 42), (block_count,), 0, L).astype(jnp.int32)
    forced = jnp.where(block_ids == block_count - 1, L - 1, free_value)
    forced = jnp.where(block_ids == 0, 0, forced).astype(jnp.int32)

    def one_block(block_key, fixed_value):
        others = jax.random.permutation(block_key, L - 1)[:SAMP_DEV - 1].astype(jnp.int32)
        others = others + (others >= fixed_value).astype(jnp.int32)
        return jnp.concatenate([fixed_value[None], others])
    offsets = jax.vmap(one_block)(block_keys, forced)
    return (block_ids[:, None] * L + offsets).reshape(-1).astype(jnp.int32)


def setup_inputs(seed: int = 0) -> dict:
    seeds = jax.random.split(jax.random.key(seed), 5)
    mat = draw_mat(jax.random.fold_in(seeds[4], 71), 0)
    signs = draw_signs(jax.random.fold_in(seeds[4], 71), 0)
    picks = draw_picks(jax.random.fold_in(seeds[4], 71), 0)
    rhs = draw_rhs(jax.random.fold_in(seeds[4], 71), 0)
    return dict(mat=mat, signs=signs, picks=picks, rhs=rhs)


def walsh_rows(columns):
    total = columns.shape[0]
    col_count = columns.shape[1]
    half_span = 1
    while half_span < total:
        paired = columns.reshape(total // (2 * half_span), 2, half_span, col_count)
        upper_half = paired[:, 0] + paired[:, 1]
        lower_half = paired[:, 0] - paired[:, 1]
        columns = jnp.stack([upper_half, lower_half], axis=1).reshape(total, col_count)
        half_span = half_span * 2
    return columns

def reference(mat, signs, picks, rhs):
    total = mat.shape[0]
    samples = picks.shape[0]
    signed = mat * signs.astype(jnp.float32)[:, None]
    block_width = min(128, N)
    stacked = signed.reshape(total, N // block_width, block_width).transpose(1, 0, 2)

    def sketch_block(columns):
        return walsh_rows(columns)[picks]
    picked = lax.map(sketch_block, stacked)
    sketch = picked.transpose(1, 0, 2).reshape(samples, N) * (1.0 / math.sqrt(samples))
    gram = jnp.dot(sketch.T, sketch, precision=lax.Precision.HIGHEST)
    lower = jnp.linalg.cholesky(gram)
    beta = jnp.sqrt(lax.optimization_barrier(jnp.sum(rhs * rhs, axis=0)))
    atb = jnp.dot(mat.T, rhs, precision=lax.Precision.HIGHEST)
    lifted = lax.linalg.triangular_solve(lower, atb, left_side=True, lower=True) / beta
    alpha = jnp.sqrt(lax.optimization_barrier(jnp.sum(lifted * lifted, axis=0)))
    unit = lifted / alpha
    direction = lax.linalg.triangular_solve(lower, unit, left_side=True, lower=True, transpose_a=True)
    image = jnp.dot(mat, direction, precision=lax.Precision.HIGHEST)
    pushed = image - alpha / beta * rhs
    gamma = jnp.sqrt(lax.optimization_barrier(jnp.sum(pushed * pushed, axis=0)))
    coef = beta * alpha / (alpha * alpha + gamma * gamma)
    return (lower.T, direction * coef, rhs - image * coef)
```

```python
import functools

import jax
import jax.numpy as jnp
from jax import lax
from jax.experimental import pallas as pl
from jax.experimental.pallas import tpu as pltpu
from jax.sharding import PartitionSpec as P

exact_mode = lax.Precision.HIGHEST
TILE = 128
SUB = 8
AXES = ("rows", "grp")


def walsh_table(table_order, piece=1):
    counter = lax.iota(jnp.int32, table_order)
    outer = counter // piece
    common_bits = outer[:, None] & outer[None, :]
    parity = jnp.zeros((table_order, table_order), jnp.int32)
    for bit_pos in range(max((table_order // piece).bit_length() - 1, 0)):
        parity = parity + (common_bits >> bit_pos & 1)
    table = jnp.where(parity % 2 == 0, 1.0, -1.0).astype(jnp.float32)
    inner = counter % piece
    return jnp.where(inner[:, None] == inner[None, :], table, 0.0)


def dot_tt(a, b):
    return lax.dot_general(a, b, (((0,), (0,)), ((), ())), precision=exact_mode,
                           preferred_element_type=jnp.float32)


def dot_nn(a, b):
    return lax.dot_general(a, b, (((1,), (0,)), ((), ())), precision=exact_mode,
                           preferred_element_type=jnp.float32)


def factor_tile(block):
    groups = TILE // SUB
    lane = lax.broadcasted_iota(jnp.int32, (SUB, TILE), 1)
    sub = lax.broadcasted_iota(jnp.int32, (SUB, TILE), 0)
    wide = (SUB, TILE)
    left = [block[SUB * g:SUB * (g + 1), :] for g in range(groups)]
    right = [(lane == sub + SUB * g).astype(jnp.float32) for g in range(groups)]
    for g in range(groups):
        base = SUB * g
        cols = [jnp.broadcast_to(left[g][:, base + t:base + t + 1], wide) for t in range(SUB)]
        pivots, invs, rows, rows_e = [], [], [], []
        for s in range(SUB):
            scal = [jnp.broadcast_to(cols[t][s:s + 1, :], wide) for t in range(s, SUB)]
            inv = 1.0 / scal[0]
            mult = jnp.where(sub > s, cols[s] * inv, 0.0)
            for t in range(s + 1, SUB):
                cols[t] = cols[t] - mult * scal[t - s]
            row = jnp.broadcast_to(left[g][s:s + 1, :], wide)
            row_e = jnp.broadcast_to(right[g][s:s + 1, :], wide)
            left[g] = left[g] - mult * row
            right[g] = right[g] - mult * row_e
            pivots.append(scal)
            invs.append(inv)
            rows.append(row)
            rows_e.append(row_e)
        for h in range(g + 1, groups):
            cols = [jnp.broadcast_to(left[h][:, base + t:base + t + 1], wide) for t in range(SUB)]
            for s in range(SUB):
                mult = cols[s] * invs[s]
                for t in range(s + 1, SUB):
                    cols[t] = cols[t] - mult * pivots[s][t - s]
                left[h] = left[h] - mult * rows[s]
                right[h] = right[h] - mult * rows_e[s]
    for g in range(groups):
        pivot = jnp.sum(jnp.where(lane == sub + SUB * g, left[g], 0.0), axis=1, keepdims=True)
        root = jnp.sqrt(pivot)
        left[g] = jnp.where(lane >= sub + SUB * g, left[g] / root, 0.0)
        right[g] = jnp.where(lane <= sub + SUB * g, right[g] / root, 0.0)
    return jnp.concatenate(left, axis=0), jnp.concatenate(right, axis=0)


def split2(x):
    hi = x.astype(jnp.bfloat16)
    return hi, (x - hi.astype(jnp.float32)).astype(jnp.bfloat16)


def dot_pairs(a, b, dims):
    def one(x, y):
        return lax.dot_general(x, y, (dims, ((), ())), preferred_element_type=jnp.float32)
    return one(a[0], b[0]) + (one(a[0], b[1]) + one(a[1], b[0]))


NN = ((1,), (0,))
TT = ((0,), (0,))


def eliminate(tiles, work, inverse, high, low, ready=None):
    n = tiles * TILE

    def step(k, carry):
        here = pl.ds(pl.multiple_of(k * TILE, TILE), TILE)
        for kk in range(tiles):
            if ready is None and kk == 0:
                continue

            @pl.when(k == kk)
            def _(kk=kk):
                if ready is not None:
                    ready(kk)
                if kk:
                    at = kk * TILE
                    own = (high[:at, at:at + TILE], low[:at, at:at + TILE])
                    rest = (high[:at, at:], low[:at, at:])
                    work[at:at + TILE, at:] = work[at:at + TILE, at:] - dot_pairs(own, rest, TT)

        upper, inv = factor_tile(work[here, here])
        inverse[here, :] = inv
        work[here, here] = upper
        for kk in range(tiles):
            @pl.when(k == kk)
            def _(kk=kk):
                at = kk * TILE
                panel = dot_pairs(split2(inverse[at:at + TILE, :]), split2(work[at:at + TILE, at + TILE:]), NN)
                work[at:at + TILE, at + TILE:] = panel
                panel_high, panel_low = split2(panel)
                high[at:at + TILE, at + TILE:] = panel_high
                low[at:at + TILE, at + TILE:] = panel_low
        return carry

    lax.fori_loop(0, tiles, step, 0)


def back_solve(tiles, work, inverse, high, low, direction_ref, dir_high, dir_low):
    n = tiles * TILE
    for k in range(tiles - 1, -1, -1):
        at = k * TILE
        rest = work[at:at + TILE, n:]
        if k < tiles - 1:
            row = (high[at:at + TILE, at + TILE:n], low[at:at + TILE, at + TILE:n])
            rest = rest - dot_pairs(row, (dir_high[at + TILE:, :], dir_low[at + TILE:, :]), NN)
        part = dot_pairs(split2(inverse[at:at + TILE, :]), split2(rest), TT)
        direction_ref[at:at + TILE, :] = part
        part_high, part_low = split2(part)
        dir_high[at:at + TILE, :] = part_high
        dir_low[at:at + TILE, :] = part_low


def factor_kernel(packed_ref, atb_ref, squares_ref, tri_ref, direction_ref, alpha_ref,
                  work, inverse, high, low, dir_high, dir_low):
    n = tri_ref.shape[0]
    tiles = n // TILE
    offset = 0
    for i in range(tiles):
        for j in range(i, tiles):
            work[i * TILE:(i + 1) * TILE, j * TILE:(j + 1) * TILE] = packed_ref[offset:offset + TILE, :]
            offset += TILE
        if i:
            work[i * TILE:(i + 1) * TILE, :i * TILE] = jnp.zeros((TILE, i * TILE), jnp.float32)
    work[:, n:] = atb_ref[...]
    eliminate(tiles, work, inverse, high, low)
    tri_ref[...] = work[:, :n]
    beta = jnp.sqrt(squares_ref[0:1, :])
    lifted = work[:, n:] / beta
    alpha = jnp.sqrt(jnp.sum(lifted * lifted, axis=0, keepdims=True))
    alpha_ref[...] = jnp.broadcast_to(alpha, alpha_ref.shape)
    work[:, n:] = lifted / alpha
    back_solve(tiles, work, inverse, high, low, direction_ref, dir_high, dir_low)


def factor_and_solve(packed, atb, squares):
    n, k = atb.shape
    return pl.pallas_call(
        factor_kernel,
        out_shape=(
            jax.ShapeDtypeStruct((n, n), jnp.float32),
            jax.ShapeDtypeStruct((n, k), jnp.float32),
            jax.ShapeDtypeStruct((SUB, k), jnp.float32),
        ),
        in_specs=[pl.BlockSpec(memory_space=pltpu.VMEM)] * 3,
        out_specs=(pl.BlockSpec(memory_space=pltpu.VMEM),) * 3,
        scratch_shapes=[
            pltpu.VMEM((n, n + k), jnp.float32),
            pltpu.VMEM((n, TILE), jnp.float32),
            pltpu.VMEM((n, n + k), jnp.bfloat16),
            pltpu.VMEM((n, n + k), jnp.bfloat16),
            pltpu.VMEM((n, k), jnp.bfloat16),
            pltpu.VMEM((n, k), jnp.bfloat16),
        ],
        compiler_params=pltpu.CompilerParams(vmem_limit_bytes=48 * 1024 * 1024),
        name="factor_and_solve",
    )(packed, atb, squares)


def shards(mat, signs, picks, rhs):
    row_count, n = mat.shape
    devices = lax.axis_size("rows") * lax.axis_size("grp")
    samples = picks.shape[0] * devices
    piece = row_count // devices

    atb_part = dot_tt(mat, rhs)
    atb = lax.psum(atb_part, AXES)

    local_rows = lax.iota(jnp.int32, row_count)
    hits = jnp.sum(
        ((picks % row_count)[:, None] == local_rows[None, :]).astype(jnp.float32), axis=0
    ) * (1.0 / samples)
    squares_part = jnp.sum(rhs * rhs, axis=0, keepdims=True)
    small = jnp.concatenate(
        [
            jnp.broadcast_to(squares_part, (devices, rhs.shape[1])),
            hits.reshape(devices, piece),
        ],
        axis=1,
    )
    small = lax.all_to_all(small, AXES, 0, 0, tiled=True)
    hits = small[:, rhs.shape[1]:]
    squares = jnp.broadcast_to(
        jnp.sum(small[:, :rhs.shape[1]], axis=0, keepdims=True), (SUB, rhs.shape[1])
    )

    mixed = mat * signs.astype(jnp.float32)[:, None]
    mixed = dot_nn(walsh_table(row_count), mixed)
    if piece % SUB == 0:
        turned = lax.all_to_all(mixed, AXES, 0, 0, tiled=True)
    else:
        turned = mixed.reshape(devices, piece * n // TILE, TILE)
        turned = lax.all_to_all(turned, AXES, 0, 0, tiled=True).reshape(row_count, n)
    turned = dot_nn(walsh_table(row_count, piece), turned)
    weighted = turned * hits.reshape(row_count, 1)
    strips = [
        dot_tt(weighted[:, at:at + TILE], turned[:, at:]) for at in range(0, n, TILE)
    ]
    tiles = [
        strip[:, at:at + TILE] for strip in strips for at in range(0, strip.shape[1], TILE)
    ]
    packed = lax.psum(jnp.concatenate(tiles, axis=0), AXES)

    tri, direction, alpha = factor_and_solve(packed, atb, squares)
    alpha = alpha[0]
    beta = jnp.sqrt(squares[0])
    image = dot_nn(mat, direction)
    pushed = image - alpha / beta * rhs
    gamma_part = jnp.sum(pushed * pushed, axis=0, keepdims=True)
    gamma_parts = lax.all_to_all(
        jnp.broadcast_to(gamma_part, (devices, rhs.shape[1])), AXES, 0, 0, tiled=True
    )
    gamma_sq = jnp.sum(gamma_parts, axis=0)
    coef = beta * alpha / (alpha * alpha + gamma_sq)
    return (tri, direction * coef, rhs - image * coef)


def solution(mesh):
    return jax.shard_map(
        shards,
        mesh=mesh,
        in_specs=(P(AXES, None), P(AXES), P(AXES), P(AXES, None)),
        out_specs=(P(), P(), P(AXES, None)),
        check_vma=False,
    )
```

```python
import functools
import math

import jax
import jax.numpy as jnp
from jax import lax
from jax.experimental import pallas as pl
from jax.experimental.pallas import tpu as pltpu
from jax.sharding import PartitionSpec as P

TILE = 128
SUB = 8
AXES = ("rows", "grp")
MESH = pl.DeviceIdType.MESH


def place():
    grp = lax.axis_size("grp")
    return lax.axis_index("rows") * grp + lax.axis_index("grp")


def coords(index):
    grp = lax.axis_size("grp")
    return (index // grp, lax.rem(index, grp))


def send(src, dst, send_sem, recv_sem, target):
    pltpu.make_async_remote_copy(src_ref=src, dst_ref=dst, send_sem=send_sem, recv_sem=recv_sem,
                                 device_id=coords(target), device_id_type=MESH).start()


def await_bytes(ref, sem):
    pltpu.make_async_copy(ref, ref, sem).wait()


def greet(devices, me):
    barrier = pltpu.get_barrier_semaphore()

    def one(d, carry):
        pl.semaphore_signal(barrier, inc=1, device_id=coords(lax.rem(me + d, devices)), device_id_type=MESH)
        return carry

    lax.fori_loop(1, devices, one, 0)
    return barrier


def loop(start, stop, body):
    def one(i, carry):
        body(i)
        return carry

    lax.fori_loop(start, stop, one, 0)


def factor_tile(block):
    groups = TILE // SUB
    lane = lax.broadcasted_iota(jnp.int32, (SUB, TILE), 1)
    sub = lax.broadcasted_iota(jnp.int32, (SUB, TILE), 0)
    wide = (SUB, TILE)
    left = [block[SUB * g:SUB * (g + 1), :] for g in range(groups)]
    right = [(lane == sub + SUB * g).astype(jnp.float32) for g in range(groups)]
    for g in range(groups):
        base = SUB * g
        cols = [jnp.broadcast_to(left[g][:, base + t:base + t + 1], wide) for t in range(SUB)]
        pivots, invs, rows, rows_e = [], [], [], []
        for s in range(SUB):
            scal = [jnp.broadcast_to(cols[t][s:s + 1, :], wide) for t in range(s, SUB)]
            inv = 1.0 / scal[0]
            mult = jnp.where(sub > s, cols[s] * inv, 0.0)
            for t in range(s + 1, SUB):
                cols[t] = cols[t] - mult * scal[t - s]
            row = jnp.broadcast_to(left[g][s:s + 1, :], wide)
            row_e = jnp.broadcast_to(right[g][s:s + 1, :], wide)
            left[g] = left[g] - mult * row
            right[g] = right[g] - mult * row_e
            pivots.append(scal)
            invs.append(inv)
            rows.append(row)
            rows_e.append(row_e)
        for h in range(g + 1, groups):
            cols = [jnp.broadcast_to(left[h][:, base + t:base + t + 1], wide) for t in range(SUB)]
            for s in range(SUB):
                mult = cols[s] * invs[s]
                for t in range(s + 1, SUB):
                    cols[t] = cols[t] - mult * pivots[s][t - s]
                left[h] = left[h] - mult * rows[s]
                right[h] = right[h] - mult * rows_e[s]
    for g in range(groups):
        pivot = jnp.sum(jnp.where(lane == sub + SUB * g, left[g], 0.0), axis=1, keepdims=True)
        root = jnp.sqrt(pivot)
        left[g] = jnp.where(lane >= sub + SUB * g, left[g] / root, 0.0)
        right[g] = jnp.where(lane <= sub + SUB * g, right[g] / root, 0.0)
    return jnp.concatenate(left, axis=0), jnp.concatenate(right, axis=0)


def dot_tt(a, b):
    return lax.dot_general(a, b, (TT, ((), ())), preferred_element_type=jnp.float32)


def split2(x):
    hi = x.astype(jnp.bfloat16)
    return hi, (x - hi.astype(jnp.float32)).astype(jnp.bfloat16)


def dot_pairs(a, b, dims):
    def one(x, y):
        return lax.dot_general(x, y, (dims, ((), ())), preferred_element_type=jnp.float32)
    return one(a[0], b[0]) + (one(a[0], b[1]) + one(a[1], b[0]))


NN = ((1,), (0,))
TT = ((0,), (0,))


def eliminate(tiles, work, inverse, high, low, ready, panel_ready):

    def step(k, carry):
        here = pl.ds(pl.multiple_of(k * TILE, TILE), TILE)
        for kk in range(tiles):
            @pl.when(k == kk)
            def _(kk=kk):
                ready(kk)
                if kk:
                    at = kk * TILE
                    own = (high[:at, at:at + TILE], low[:at, at:at + TILE])
                    rest = (high[:at, at:], low[:at, at:])
                    work[at:at + TILE, at:] = work[at:at + TILE, at:] - dot_pairs(own, rest, TT)

        upper, inv = factor_tile(work[here, here])
        inverse[here, :] = inv
        work[here, here] = upper
        for kk in range(tiles):
            @pl.when(k == kk)
            def _(kk=kk):
                at = kk * TILE
                panel_ready(kk)
                panel = dot_pairs(split2(inverse[at:at + TILE, :]), split2(work[at:at + TILE, at + TILE:]), NN)
                work[at:at + TILE, at + TILE:] = panel
                panel_high, panel_low = split2(panel)
                high[at:at + TILE, at + TILE:] = panel_high
                low[at:at + TILE, at + TILE:] = panel_low
        return carry

    lax.fori_loop(0, tiles, step, 0)


def back_solve(tiles, work, inverse, high, low, direction_ref, dir_high, dir_low):
    n = tiles * TILE
    for k in range(tiles - 1, -1, -1):
        at = k * TILE
        rest = work[at:at + TILE, n:]
        if k < tiles - 1:
            row = (high[at:at + TILE, at + TILE:n], low[at:at + TILE, at + TILE:n])
            rest = rest - dot_pairs(row, (dir_high[at + TILE:, :], dir_low[at + TILE:, :]), NN)
        part = dot_pairs(split2(inverse[at:at + TILE, :]), split2(rest), TT)
        direction_ref[at:at + TILE, :] = part
        part_high, part_low = split2(part)
        dir_high[at:at + TILE, :] = part_high
        dir_low[at:at + TILE, :] = part_low


def tile_of(t, tiles):
    row, offset = 0, 0
    start = 0
    for r in range(1, tiles):
        start = start + tiles - r + 1
        past = (t - start + tiles * tiles) // (tiles * tiles)
        row = row + past
        offset = offset + past * (tiles - r + 1)
    return row, t - offset + row


def parity(value, bits):
    width = 1
    while width < bits:
        width *= 2
    while width > 1:
        width //= 2
        value = value ^ (value >> width)
    return value & 1


def mix_kernel(mat_ref, signs_ref, picks_ref, rhs_ref, out_ref,
               signed, dense, picks_all, table, mixed_high, mixed_low, partial, landed, sketch,
               atb_send, atb_land, picks_out, send_sem, recv_sem, layer_sem):
    devices = picks_all.shape[0]
    planes, depth, _ = landed.shape
    tiles, rows, _ = dense.shape
    samp = depth // tiles
    per = TILE // samp
    me = place()
    z, q = me // tiles, lax.rem(me, tiles)
    scale = 1.0 / math.sqrt(samp * devices)

    barrier = greet(devices, me)
    sign = signs_ref[...]
    for p in range(tiles):
        signed[p] = mat_ref[:, p * TILE:(p + 1) * TILE] * sign
    picks_out[...] = picks_ref[...]
    picks_all[me] = picks_ref[...]
    pl.semaphore_wait(barrier, devices - 1)

    def send_picks(d):
        send(picks_out, picks_all.at[me], send_sem.at[0], recv_sem.at[0], lax.rem(me + d, devices))

    loop(1, devices, send_picks)

    def send_dense(d):
        p = lax.rem(q + d, tiles)
        send(signed.at[p], dense.at[q], send_sem.at[1], recv_sem.at[1], z * tiles + p)

    loop(1, tiles, send_dense)
    dense[q] = signed[q]

    rhs = rhs_ref[...]
    rhs_pair = split2(rhs)
    squares = jnp.broadcast_to(jnp.sum(rhs * rhs, axis=0, keepdims=True), (SUB, TILE))

    def atb_tile(p):
        at = pl.multiple_of(p * TILE, TILE)
        atb_send[p, :TILE, :] = dot_pairs(split2(mat_ref[:, pl.ds(at, TILE)]), rhs_pair, TT)
        atb_send[p, TILE:, :] = squares

    loop(0, tiles, atb_tile)
    atb_land[q] = atb_send[q]

    def send_atb(d):
        p = lax.rem(q + d, tiles)
        send(atb_send.at[p], atb_land.at[q], send_sem.at[2], recv_sem.at[2], z * tiles + p)

    loop(1, tiles, send_atb)

    await_bytes(picks_all.at[pl.ds(0, devices - 1)], recv_sem.at[0])
    lane = lax.broadcasted_iota(jnp.int32, (1, TILE), 1)

    def fill_table(c):
        group, qk = c // tiles, lax.rem(c, tiles)
        row = picks_all[group * per * tiles + qk]
        for e in range(1, per):
            row = jnp.where(lane >= e * samp, picks_all[(group * per + e) * tiles + qk], row)
        counter = lax.broadcasted_iota(jnp.int32, (rows, TILE), 0)
        odd = parity(counter & row, (rows - 1).bit_length())
        table[c] = (1 - 2 * odd).astype(jnp.float32).astype(jnp.bfloat16)

    loop(0, planes // per * tiles, fill_table)

    await_bytes(dense.at[pl.ds(0, tiles - 1)], recv_sem.at[1])
    chunk = 32

    def butterfly(c):
        here = pl.ds(pl.multiple_of(c * chunk, chunk), chunk)
        parts = [dense[d, here, :] for d in range(tiles)]
        span = 1
        while span < tiles:
            parts = [parts[d] + parts[d + span] if d // span % 2 == 0 else parts[d - span] - parts[d]
                     for d in range(tiles)]
            span *= 2
        for d in range(tiles):
            high, low = split2(parts[d])
            mixed_high[d, here, :] = high
            mixed_low[d, here, :] = low

    loop(0, rows // chunk, butterfly)

    def project(qk):
        here = pl.ds(pl.multiple_of(qk * samp, samp), samp)
        for group in range(planes // per):
            rows_of = table[group * tiles + qk]
            block = dot_tt(rows_of, mixed_high[qk]) + dot_tt(rows_of, mixed_low[qk])
            for e in range(per):
                zk = group * per + e
                odd = 0
                for bit in range(planes.bit_length() - 1):
                    if zk >> bit & 1:
                        odd = odd + lax.rem(z // (1 << bit), 2)
                flip = 1.0 - 2.0 * jnp.asarray(lax.rem(jnp.asarray(odd, jnp.int32), 2), jnp.float32)
                partial[zk, here, :] = block[e * samp:(e + 1) * samp, :] * (flip * scale)
        landed[z, here, :] = partial[z, here, :]

        def send_layer(d):
            zk = lax.rem(z + d, planes)
            send(partial.at[zk, here], landed.at[z, here], send_sem.at[3], layer_sem.at[qk], zk * tiles + q)

        loop(1, planes, send_layer)

    loop(0, tiles, project)

    def combine(qk):
        here = pl.ds(pl.multiple_of(qk * samp, samp), samp)
        await_bytes(landed.at[pl.ds(0, planes - 1), here], layer_sem.at[qk])
        sketch[q, here, :] = jnp.sum(landed[:, here, :], axis=0)

        def send_sketch(d):
            p = lax.rem(q + d, tiles)
            send(sketch.at[q, here], sketch.at[q, here], send_sem.at[4], recv_sem.at[4], z * tiles + p)

        loop(1, tiles, send_sketch)

    loop(0, tiles, combine)

    await_bytes(atb_land.at[pl.ds(0, tiles - 1)], recv_sem.at[2])
    slots = out_ref.shape[0] - 1
    out_ref[slots] = jnp.sum(atb_land[...], axis=0)

    await_bytes(sketch.at[pl.ds(0, tiles - 1)], recv_sem.at[4])

    def gram_tile(s):
        t = jnp.minimum(s * tiles + q, tiles * (tiles + 1) // 2 - 1)
        i, j = tile_of(t, tiles)
        out_ref[s, :TILE, :] = dot_pairs(split2(sketch[i]), split2(sketch[j]), TT)
        out_ref[s, TILE:, :] = jnp.zeros((SUB, TILE), jnp.float32)

    loop(0, slots, gram_tile)

    def drain(d):
        await_bytes(picks_out, send_sem.at[0])

    loop(1, devices, drain)
    await_bytes(dense.at[pl.ds(0, tiles - 1)], send_sem.at[1])
    await_bytes(atb_land.at[pl.ds(0, tiles - 1)], send_sem.at[2])
    await_bytes(partial.at[pl.ds(0, planes - 1)], send_sem.at[3])
    await_bytes(sketch.at[pl.ds(0, tiles - 1)], send_sem.at[4])


def mix(mat, signs, picks, rhs, devices):
    rows, n = mat.shape
    tiles = n // TILE
    samp = picks.shape[0]
    planes = devices // tiles
    per = TILE // samp
    slots = (tiles * (tiles + 1) // 2 + tiles - 1) // tiles
    vmem = pl.BlockSpec(memory_space=pltpu.VMEM)
    f32, bf16 = jnp.float32, jnp.bfloat16
    sign_column = signs.astype(f32).reshape(rows, 1)
    picks_row = jnp.tile(picks % rows, per).reshape(1, TILE)
    return pl.pallas_call(
        mix_kernel,
        out_shape=jax.ShapeDtypeStruct((slots + 1, TILE + SUB, TILE), f32),
        in_specs=[vmem] * 4,
        out_specs=vmem,
        scratch_shapes=[
            pltpu.VMEM((tiles, rows, TILE), f32),
            pltpu.VMEM((tiles, rows, TILE), f32),
            pltpu.VMEM((devices, 1, TILE), jnp.int32),
            pltpu.VMEM((planes // per * tiles, rows, TILE), bf16),
            pltpu.VMEM((tiles, rows, TILE), bf16),
            pltpu.VMEM((tiles, rows, TILE), bf16),
            pltpu.VMEM((planes, tiles * samp, TILE), f32),
            pltpu.VMEM((planes, tiles * samp, TILE), f32),
            pltpu.VMEM((tiles, tiles * samp, TILE), f32),
            pltpu.VMEM((tiles, TILE + SUB, TILE), f32),
            pltpu.VMEM((tiles, TILE + SUB, TILE), f32),
            pltpu.VMEM((1, TILE), jnp.int32),
            pltpu.SemaphoreType.DMA((5,)),
            pltpu.SemaphoreType.DMA((5,)),
            pltpu.SemaphoreType.DMA((tiles,)),
        ],
        compiler_params=pltpu.CompilerParams(
            collective_id=0, has_side_effects=True, vmem_limit_bytes=56 * 1024 * 1024),
        name="mix",
    )(mat, sign_column, picks_row, rhs)


def solve_kernel(part_ref, mat_ref, rhs_ref, tri_ref, solution_ref, residual_ref,
                 landed, gathered, work, inverse, high, low, mat_high, mat_low, direction, dir_high, dir_low,
                 squares, gamma_out, gamma_all, send_sem, layer_sem, plane_sem, gamma_sem, tri_sem):
    planes = landed.shape[0]
    tiles, slots = gathered.shape[0], gathered.shape[1] - 1
    n = tiles * TILE
    devices = planes * tiles
    me = place()
    z, q = me // tiles, lax.rem(me, tiles)
    height = [TILE] * slots + [TILE + SUB]
    order = [0, slots] + list(range(1, slots))

    barrier = greet(devices, me)
    for i in range(1, tiles):
        work[i * TILE:(i + 1) * TILE, :i * TILE] = jnp.zeros((TILE, i * TILE), jnp.float32)
    for s in range(slots + 1):
        landed[z, s] = part_ref[s]
    pl.semaphore_wait(barrier, devices - 1)
    for s in order:
        def send_layer(d, s=s):
            zk = lax.rem(z + d, planes)
            send(part_ref.at[s, :height[s]], landed.at[z, s, :height[s]], send_sem.at[0], layer_sem.at[s],
                 zk * tiles + q)

        loop(1, planes, send_layer)

    mat_high[...], mat_low[...] = split2(mat_ref[...])

    def advance(s):
        await_bytes(landed.at[pl.ds(0, planes - 1), s, :height[s]], layer_sem.at[s])
        total = jnp.sum(landed[:, s, :height[s], :], axis=0)
        gathered[q, s] = total[:TILE]
        if s == slots:
            squares[...] = total[TILE:]

        def send_plane(d):
            p = lax.rem(q + d, tiles)
            send(gathered.at[q, s], gathered.at[q, s], send_sem.at[1], plane_sem.at[s], z * tiles + p)

        loop(1, tiles, send_plane)

    def take(s):
        await_bytes(gathered.at[pl.ds(0, tiles - 1), s], plane_sem.at[s])
        for p in range(tiles):
            if s == slots:
                work[p * TILE:(p + 1) * TILE, n:] = gathered[p, s]
            elif s * tiles + p < tiles * (tiles + 1) // 2:
                i, j = tile_of(s * tiles + p, tiles)
                work[i * TILE:(i + 1) * TILE, j * TILE:(j + 1) * TILE] = gathered[p, s]

    last = [tile_of_end(k, tiles) // tiles for k in range(tiles)]
    moves, panel_moves = [[] for _ in range(tiles)], [[] for _ in range(tiles)]
    moves[0] = [(advance, 0), (advance, slots), (take, 0)]
    panel_moves[0] = [(advance, 1), (take, slots)]
    taken, sent = 0, 1
    for k in range(1, tiles):
        want = last[min(k + 1, tiles - 1)]
        while sent < want:
            sent += 1
            moves[k].append((advance, sent))
        while taken < last[k]:
            taken += 1
            moves[k].append((take, taken))

    def run(todo):
        for action, s in todo:
            action(s)

    def ready(k):
        if k:
            done = slice((k - 1) * TILE, k * TILE)
            pltpu.make_async_copy(work.at[done, :n], tri_ref.at[done], tri_sem).start()
        run(moves[k])

    eliminate(tiles, work, inverse, high, low, ready, lambda k: run(panel_moves[k]))
    final = slice(n - TILE, n)
    pltpu.make_async_copy(work.at[final, :n], tri_ref.at[final], tri_sem).start()

    beta = jnp.sqrt(squares[0:1, :])
    lifted = work[:, n:] / beta
    alpha = jnp.sqrt(jnp.sum(lifted * lifted, axis=0, keepdims=True))
    work[:, n:] = lifted / alpha
    back_solve(tiles, work, inverse, high, low, direction, dir_high, dir_low)

    rhs = rhs_ref[...]
    image = dot_pairs((mat_high[...], mat_low[...]), (dir_high[...], dir_low[...]), NN)
    pushed = image - alpha / beta * rhs
    gamma_out[...] = jnp.sum(pushed * pushed, axis=0, keepdims=True)
    gamma_all[me] = gamma_out[...]

    def send_gamma(d):
        send(gamma_out, gamma_all.at[me], send_sem.at[2], gamma_sem, lax.rem(me + d, devices))

    loop(1, devices, send_gamma)
    await_bytes(gamma_all.at[pl.ds(0, devices - 1)], gamma_sem)
    gamma = jnp.sqrt(jnp.sum(gamma_all[...], axis=0))
    coef = beta * alpha / (alpha * alpha + gamma * gamma)
    solution_ref[...] = direction[...] * coef
    residual_ref[...] = rhs - image * coef

    for s in range(slots + 1):
        await_bytes(landed.at[pl.ds(0, planes - 1), s, :height[s]], send_sem.at[0])
        await_bytes(gathered.at[pl.ds(0, tiles - 1), s], send_sem.at[1])
    await_bytes(gamma_all.at[pl.ds(0, devices - 1)], send_sem.at[2])
    pltpu.make_async_copy(work.at[:, :n], tri_ref, tri_sem).wait()


def tile_of_end(row, tiles):
    return sum(tiles - r for r in range(row + 1)) - 1


def solve(part, mat, rhs, devices):
    rows, n = mat.shape
    tiles = n // TILE
    planes = devices // tiles
    slots = part.shape[0] - 1
    vmem = pl.BlockSpec(memory_space=pltpu.VMEM)
    f32, bf16 = jnp.float32, jnp.bfloat16
    return pl.pallas_call(
        solve_kernel,
        out_shape=(
            jax.ShapeDtypeStruct((n, n), f32),
            jax.ShapeDtypeStruct((n, TILE), f32),
            jax.ShapeDtypeStruct((rows, TILE), f32),
        ),
        in_specs=[vmem] * 3,
        out_specs=(pl.BlockSpec(memory_space=pl.ANY), vmem, vmem),
        scratch_shapes=[
            pltpu.VMEM((planes, slots + 1, TILE + SUB, TILE), f32),
            pltpu.VMEM((tiles, slots + 1, TILE, TILE), f32),
            pltpu.VMEM((n, n + TILE), f32),
            pltpu.VMEM((n, TILE), f32),
            pltpu.VMEM((n, n + TILE), bf16),
            pltpu.VMEM((n, n + TILE), bf16),
            pltpu.VMEM((rows, n), bf16),
            pltpu.VMEM((rows, n), bf16),
            pltpu.VMEM((n, TILE), f32),
            pltpu.VMEM((n, TILE), bf16),
            pltpu.VMEM((n, TILE), bf16),
            pltpu.VMEM((SUB, TILE), f32),
            pltpu.VMEM((1, TILE), f32),
            pltpu.VMEM((devices, 1, TILE), f32),
            pltpu.SemaphoreType.DMA((3,)),
            pltpu.SemaphoreType.DMA((slots + 1,)),
            pltpu.SemaphoreType.DMA((slots + 1,)),
            pltpu.SemaphoreType.DMA,
            pltpu.SemaphoreType.DMA,
        ],
        compiler_params=pltpu.CompilerParams(
            collective_id=1, has_side_effects=True, vmem_limit_bytes=56 * 1024 * 1024),
        name="factor_and_solve",
    )(part, mat, rhs)


def shards(mat, signs, picks, rhs):
    devices = lax.axis_size("rows") * lax.axis_size("grp")
    part = mix(mat, signs, picks, rhs, devices)
    return solve(part, mat, rhs, devices)


def solution(mesh):
    return jax.shard_map(
        shards,
        mesh=mesh,
        in_specs=(P(AXES, None), P(AXES), P(AXES), P(AXES, None)),
        out_specs=(P(), P(), P(AXES, None)),
        check_vma=False,
    )
```

```python
import functools
import math

import jax
import jax.numpy as jnp
from jax import lax
from jax.experimental import pallas as pl
from jax.experimental.pallas import tpu as pltpu
from jax.sharding import PartitionSpec as P

TILE = 128
SUB = 8
AXES = ("rows", "grp")
MESH = pl.DeviceIdType.MESH


def place():
    grp = lax.axis_size("grp")
    return lax.axis_index("rows") * grp + lax.axis_index("grp")


def coords(index):
    grp = lax.axis_size("grp")
    return (index // grp, lax.rem(index, grp))


def send(src, dst, send_sem, recv_sem, target):
    pltpu.make_async_remote_copy(src_ref=src, dst_ref=dst, send_sem=send_sem, recv_sem=recv_sem,
                                 device_id=coords(target), device_id_type=MESH).start()


def await_bytes(ref, sem):
    pltpu.make_async_copy(ref, ref, sem).wait()


def greet(devices, me):
    barrier = pltpu.get_barrier_semaphore()

    def one(d, carry):
        pl.semaphore_signal(barrier, inc=1, device_id=coords(lax.rem(me + d, devices)), device_id_type=MESH)
        return carry

    lax.fori_loop(1, devices, one, 0)
    return barrier


def loop(start, stop, body):
    def one(i, carry):
        body(i)
        return carry

    lax.fori_loop(start, stop, one, 0)


def factor_tile(block):
    groups = TILE // SUB
    lane = lax.broadcasted_iota(jnp.int32, (SUB, TILE), 1)
    sub = lax.broadcasted_iota(jnp.int32, (SUB, TILE), 0)
    wide = (SUB, TILE)
    left = [block[SUB * g:SUB * (g + 1), :] for g in range(groups)]
    right = [(lane == sub + SUB * g).astype(jnp.float32) for g in range(groups)]
    for g in range(groups):
        base = SUB * g
        cols = [jnp.broadcast_to(left[g][:, base + t:base + t + 1], wide) for t in range(SUB)]
        pivots, invs, rows, rows_e = [], [], [], []
        for s in range(SUB):
            scal = [jnp.broadcast_to(cols[t][s:s + 1, :], wide) for t in range(s, SUB)]
            inv = 1.0 / scal[0]
            mult = jnp.where(sub > s, cols[s] * inv, 0.0)
            for t in range(s + 1, SUB):
                cols[t] = cols[t] - mult * scal[t - s]
            row = jnp.broadcast_to(left[g][s:s + 1, :], wide)
            row_e = jnp.broadcast_to(right[g][s:s + 1, :], wide)
            left[g] = left[g] - mult * row
            right[g] = right[g] - mult * row_e
            pivots.append(scal)
            invs.append(inv)
            rows.append(row)
            rows_e.append(row_e)
        for h in range(g + 1, groups):
            cols = [jnp.broadcast_to(left[h][:, base + t:base + t + 1], wide) for t in range(SUB)]
            for s in range(SUB):
                mult = cols[s] * invs[s]
                for t in range(s + 1, SUB):
                    cols[t] = cols[t] - mult * pivots[s][t - s]
                left[h] = left[h] - mult * rows[s]
                right[h] = right[h] - mult * rows_e[s]
    for g in range(groups):
        pivot = jnp.sum(jnp.where(lane == sub + SUB * g, left[g], 0.0), axis=1, keepdims=True)
        root = jnp.sqrt(pivot)
        left[g] = jnp.where(lane >= sub + SUB * g, left[g] / root, 0.0)
        right[g] = jnp.where(lane <= sub + SUB * g, right[g] / root, 0.0)
    return jnp.concatenate(left, axis=0), jnp.concatenate(right, axis=0)


def dot_tt(a, b):
    return lax.dot_general(a, b, (TT, ((), ())), preferred_element_type=jnp.float32)


def split2(x):
    hi = x.astype(jnp.bfloat16)
    return hi, (x - hi.astype(jnp.float32)).astype(jnp.bfloat16)


def dot_pairs(a, b, dims):
    def one(x, y):
        return lax.dot_general(x, y, (dims, ((), ())), preferred_element_type=jnp.float32)
    return one(a[0], b[0]) + (one(a[0], b[1]) + one(a[1], b[0]))


NN = ((1,), (0,))
TT = ((0,), (0,))


def eliminate(tiles, tri_ref, lift, inverse, high, low, ready, panel_ready):
    n = tiles * TILE

    def step(k, carry):
        here = pl.ds(pl.multiple_of(k * TILE, TILE), TILE)
        for kk in range(tiles):
            @pl.when(k == kk)
            def _(kk=kk):
                ready(kk)
                if kk:
                    at = kk * TILE
                    rows = slice(at, at + TILE)
                    own = (high[:at, rows], low[:at, rows])
                    change = dot_pairs(own, (high[:at, at:], low[:at, at:]), TT)
                    tri_ref[rows, at:] = tri_ref[rows, at:] - change[:, :n - at]
                    lift[rows, :] = lift[rows, :] - change[:, n - at:]

        upper, inv = factor_tile(tri_ref[here, here])
        inverse[here, :] = inv
        tri_ref[here, here] = upper
        for kk in range(tiles):
            @pl.when(k == kk)
            def _(kk=kk):
                panel_ready(kk)
                rows = slice(kk * TILE, (kk + 1) * TILE)
                right = (kk + 1) * TILE
                rest = jnp.concatenate([tri_ref[rows, right:], lift[rows, :]], axis=1) if right < n else lift[rows, :]
                panel = dot_pairs(split2(inverse[rows, :]), split2(rest), NN)
                if right < n:
                    tri_ref[rows, right:] = panel[:, :n - right]
                lift[rows, :] = panel[:, n - right:]
                high[rows, right:], low[rows, right:] = split2(panel)
        return carry

    lax.fori_loop(0, tiles, step, 0)


def back_solve(tiles, lift, inverse, high, low, direction, dir_high, dir_low):
    n = tiles * TILE
    for k in range(tiles - 1, -1, -1):
        rows = slice(k * TILE, (k + 1) * TILE)
        right = (k + 1) * TILE
        rest = lift[rows, :]
        if right < n:
            rest = rest - dot_pairs((high[rows, right:n], low[rows, right:n]), (dir_high[right:, :], dir_low[right:, :]), NN)
        part = dot_pairs(split2(inverse[rows, :]), split2(rest), TT)
        direction[rows, :] = part
        dir_high[rows, :], dir_low[rows, :] = split2(part)


def tile_of(t, tiles):
    row, offset = 0, 0
    start = 0
    for r in range(1, tiles):
        start = start + tiles - r + 1
        past = (t - start + tiles * tiles) // (tiles * tiles)
        row = row + past
        offset = offset + past * (tiles - r + 1)
    return row, t - offset + row


def parity(value, bits):
    width = 1
    while width < bits:
        width *= 2
    while width > 1:
        width //= 2
        value = value ^ (value >> width)
    return value & 1


def bit_of(value, bit):
    return lax.rem(value // (1 << bit), 2)


def step_kernel(mat_hbm, signs_ref, picks_ref, rhs_ref, tri_ref, solution_ref, residual_ref,
                mat_ref, signed, dense, picks_out, picks_all, table, mixed_high, mixed_low, partial, landed, sketch,
                atb_send, atb_land, sums, arrived, gathered, lift, inverse, high, low, mat_high, mat_low,
                direction, dir_high, dir_low, squares, gamma_out, gamma_all,
                mat_sem, send_sem, recv_sem, layer_sem, same_sem, sum_sem, tile_sem, pair_sem):
    devices = picks_all.shape[0]
    tiles, rows, _ = dense.shape
    planes, depth, _ = partial.shape
    stages = planes.bit_length() - 1
    slots = gathered.shape[1] - 1
    n = tiles * TILE
    samp = depth // tiles
    per = TILE // samp
    me = place()
    z, q = me // tiles, lax.rem(me, tiles)
    base = z * tiles
    partner = base + q + 1 - 2 * lax.rem(q, 2)
    family = [lax.rem(q + 2 * d, tiles) for d in range(1, tiles // 2)]
    across = [(z + (1 - 2 * bit_of(z, b)) * (1 << b)) * tiles + q for b in range(stages)]
    scale = 1.0 / math.sqrt(samp * devices)
    height = [TILE] * slots + [TILE + SUB]

    fetch = pltpu.make_async_copy(mat_hbm, mat_ref, mat_sem)
    fetch.start()
    barrier = greet(devices, me)
    own_picks = jnp.concatenate([picks_ref[...]] * per, axis=1)
    picks_out[...] = own_picks
    picks_all[me] = own_picks
    bands = rows // TILE
    sign_rows = jnp.concatenate([signs_ref[...].astype(jnp.float32)] * (SUB // bands), axis=0)
    sign = jnp.transpose(sign_rows)
    fetch.wait()
    for b in range(bands):
        band = slice(b * TILE, (b + 1) * TILE)
        flip = jnp.broadcast_to(sign[:, b:b + 1], (TILE, TILE))
        for p in range(tiles):
            signed[p, band, :] = mat_ref[band, p * TILE:(p + 1) * TILE] * flip
    pl.semaphore_wait(barrier, devices - 1)

    def send_picks(d):
        send(picks_out, picks_all.at[me], send_sem.at[0], recv_sem.at[0], lax.rem(me + d, devices))

    loop(1, devices, send_picks)

    def send_dense(d):
        p = lax.rem(q + d, tiles)
        send(signed.at[p], dense.at[q], send_sem.at[1], recv_sem.at[1], base + p)

    loop(1, tiles, send_dense)
    dense[q] = signed[q]

    rhs = rhs_ref[...]
    rhs_pair = split2(rhs)
    part_squares = jnp.broadcast_to(jnp.sum(rhs * rhs, axis=0, keepdims=True), (SUB, TILE))
    mat_high[...], mat_low[...] = split2(mat_ref[...])

    def atb_tile(p):
        here = pl.ds(pl.multiple_of(p * TILE, TILE), TILE)
        atb_send[p, :TILE, :] = dot_pairs((mat_high[:, here], mat_low[:, here]), rhs_pair, TT)
        atb_send[p, TILE:, :] = part_squares

    loop(0, tiles, atb_tile)
    atb_land[q] = atb_send[q]

    for i in range(1, tiles):
        tri_ref[i * TILE:(i + 1) * TILE, :i * TILE] = jnp.zeros((TILE, i * TILE), jnp.float32)

    await_bytes(picks_all.at[pl.ds(0, devices - 1)], recv_sem.at[0])
    lane = lax.broadcasted_iota(jnp.int32, (1, TILE), 1)

    def table_of(group, qk):
        row = picks_all[group * per * tiles + qk]
        for e in range(1, per):
            row = jnp.where(lane >= e * samp, picks_all[(group * per + e) * tiles + qk], row)
        counter = lax.broadcasted_iota(jnp.int32, (rows, TILE), 0)
        odd = parity(counter & row, (rows - 1).bit_length())
        return (1 - 2 * odd).astype(jnp.float32).astype(jnp.bfloat16)

    kept = table.shape[0] > 1
    if kept:
        def fill_table(c):
            table[c] = table_of(c // tiles, lax.rem(c, tiles))

        loop(0, planes // per * tiles, fill_table)

    await_bytes(dense.at[pl.ds(0, tiles - 1)], recv_sem.at[1])

    def send_atb(d):
        p = lax.rem(q + d, tiles)
        send(atb_send.at[p], atb_land.at[q], send_sem.at[2], recv_sem.at[2], base + p)

    loop(1, tiles, send_atb)
    chunk = 32

    def butterfly(c):
        here = pl.ds(pl.multiple_of(c * chunk, chunk), chunk)
        parts = [dense[d, here, :] for d in range(tiles)]
        span = 1
        while span < tiles:
            parts = [parts[d] + parts[d + span] if d // span % 2 == 0 else parts[d - span] - parts[d]
                     for d in range(tiles)]
            span *= 2
        for d in range(tiles):
            mixed_high[d, here, :], mixed_low[d, here, :] = split2(parts[d])

    loop(0, rows // chunk, butterfly)

    sizes = [planes >> (b + 1) for b in range(stages)]
    starts = [0]
    for b in range(stages):
        starts.append(starts[b] + bit_of(z, b) * sizes[b])
    landing = [sum(sizes[:b]) for b in range(stages)]

    def send_layer(b, here, sem):
        away = starts[b] + (1 - bit_of(z, b)) * sizes[b]
        send(partial.at[pl.ds(away, sizes[b]), here], landed.at[pl.ds(landing[b], sizes[b]), here],
             send_sem.at[3], sem, across[b])

    def project(qk):
        here = pl.ds(pl.multiple_of(qk * samp, samp), samp)
        for group in range(planes // per):
            rows_of = table[group * tiles + qk] if kept else table_of(group, qk)
            block = dot_tt(rows_of, mixed_high[qk]) + dot_tt(rows_of, mixed_low[qk])
            for e in range(per):
                zk = group * per + e
                slot = sum((zk >> b & 1) * sizes[b] for b in range(stages))
                odd = jnp.int32(0)
                for b in range(stages):
                    if zk >> b & 1:
                        odd = odd + bit_of(z, b)
                flip = 1.0 - 2.0 * lax.rem(odd, 2).astype(jnp.float32)
                partial[slot, here, :] = block[e * samp:(e + 1) * samp, :] * (flip * scale)
        send_layer(0, here, layer_sem.at[0, qk])

    loop(0, tiles, project)

    def combine(b, qk):
        here = slice(qk * samp, (qk + 1) * samp)
        await_bytes(landed.at[pl.ds(landing[b], sizes[b]), here], layer_sem.at[b, qk])
        total = partial[pl.ds(starts[b + 1], sizes[b]), here, :] + landed[pl.ds(landing[b], sizes[b]), here, :]
        if b + 1 < stages:
            partial[pl.ds(starts[b + 1], sizes[b]), here, :] = total
            send_layer(b + 1, here, layer_sem.at[b + 1, qk])
            return
        sketch[q, here, :] = total[0]
        mine = sketch.at[q, here]
        for p in family:
            send(mine, mine, send_sem.at[4], same_sem.at[qk], base + p)
        send(mine, mine, send_sem.at[5], recv_sem.at[3], partner)

    def relay(qk):
        here = slice(qk * samp, (qk + 1) * samp)
        await_bytes(sketch.at[pl.ds(0, len(family)), here], same_sem.at[qk])
        for p in family:
            send(sketch.at[p, here], sketch.at[p, here], send_sem.at[5], recv_sem.at[3], partner)

    lag = 2
    for t in range(tiles + lag * stages):
        for b in range(stages):
            if 0 <= t - lag * b < tiles:
                combine(b, t - lag * b)
        if 0 <= t - lag * stages < tiles:
            relay(t - lag * stages)

    await_bytes(atb_land.at[pl.ds(0, tiles - 1)], recv_sem.at[2])
    sums[0, slots] = jnp.sum(atb_land[...], axis=0)

    def send_sum(b, s):
        send(sums.at[b, s, :height[s]], arrived.at[b, s, :height[s]], send_sem.at[6], sum_sem.at[b, s], across[b])

    await_bytes(sketch.at[pl.ds(0, tiles // 2)], recv_sem.at[3])
    order = [0, slots] + list(range(1, slots))
    for s in order:
        if s < slots:
            t = jnp.minimum(s * tiles + q, tiles * (tiles + 1) // 2 - 1)
            i, j = tile_of(t, tiles)
            sums[0, s, :TILE, :] = dot_pairs(split2(sketch[i]), split2(sketch[j]), TT)
        send_sum(0, s)

    done = set()

    def once(name, s):
        fresh = (name, s) not in done
        done.add((name, s))
        return fresh

    def add_up(b, s):
        if not once(b, s):
            return
        if b:
            add_up(b - 1, s)
        await_bytes(arrived.at[b, s, :height[s]], sum_sem.at[b, s])
        total = sums[b, s, :height[s], :] + arrived[b, s, :height[s], :]
        if b + 1 < stages:
            sums[b + 1, s, :height[s], :] = total
            send_sum(b + 1, s)
            return
        gathered[q, s] = total[:TILE]
        if s == slots:
            squares[...] = total[TILE:]
        mine = gathered.at[q, s]
        for p in family:
            send(mine, mine, send_sem.at[7], tile_sem.at[s], base + p)
        send(mine, mine, send_sem.at[8], pair_sem.at[s], partner)

    def pass_on(s):
        if not once("pass", s):
            return
        add_up(stages - 1, s)
        await_bytes(gathered.at[pl.ds(0, len(family)), s], tile_sem.at[s])
        for p in family:
            send(gathered.at[p, s], gathered.at[p, s], send_sem.at[8], pair_sem.at[s], partner)

    def take(s):
        if not once("take", s):
            return
        pass_on(s)
        await_bytes(gathered.at[pl.ds(0, tiles // 2), s], pair_sem.at[s])
        for p in range(tiles):
            if s == slots:
                lift[p * TILE:(p + 1) * TILE, :] = gathered[p, s]
            elif s * tiles + p < tiles * (tiles + 1) // 2:
                i, j = tile_of(s * tiles + p, tiles)
                tri_ref[i * TILE:(i + 1) * TILE, j * TILE:(j + 1) * TILE] = gathered[p, s]

    last = [(sum(tiles - r for r in range(k + 1)) - 1) // tiles for k in range(tiles)]

    def ready(k):
        if k == 0:
            for b in range(stages - 1):
                for s in order:
                    add_up(b, s)
            for s in order[:3]:
                add_up(stages - 1, s)
            take(0)
            return
        if k + 2 < slots:
            add_up(stages - 1, k + 2)
        for s in range(last[k] + 1):
            take(s)
        if k + 1 < slots:
            pass_on(k + 1)

    def panel_ready(k):
        if k == 0:
            pass_on(slots)
            pass_on(1)
            add_up(stages - 1, 2)
            take(slots)

    eliminate(tiles, tri_ref, lift, inverse, high, low, ready, panel_ready)

    beta = jnp.sqrt(squares[0:1, :])
    lifted = lift[...] / beta
    alpha = jnp.sqrt(jnp.sum(lifted * lifted, axis=0, keepdims=True))
    lift[...] = lifted / alpha
    back_solve(tiles, lift, inverse, high, low, direction, dir_high, dir_low)

    rhs = rhs_ref[...]
    image = dot_pairs((mat_high[...], mat_low[...]), (dir_high[...], dir_low[...]), NN)
    pushed = image - alpha / beta * rhs
    gamma_out[...] = jnp.sum(pushed * pushed, axis=0, keepdims=True)
    gamma_all[me] = gamma_out[...]

    def send_gamma(d):
        send(gamma_out, gamma_all.at[me], send_sem.at[9], recv_sem.at[4], lax.rem(me + d, devices))

    loop(1, devices, send_gamma)

    def drain(d):
        await_bytes(picks_out, send_sem.at[0])

    loop(1, devices, drain)
    await_bytes(dense.at[pl.ds(0, tiles - 1)], send_sem.at[1])
    await_bytes(atb_land.at[pl.ds(0, tiles - 1)], send_sem.at[2])
    await_bytes(partial.at[pl.ds(0, planes - 1)], send_sem.at[3])
    await_bytes(sketch.at[pl.ds(0, len(family))], send_sem.at[4])
    await_bytes(sketch.at[pl.ds(0, tiles // 2)], send_sem.at[5])
    for s in range(slots + 1):
        for b in range(stages):
            await_bytes(arrived.at[b, s, :height[s]], send_sem.at[6])
        await_bytes(gathered.at[pl.ds(0, len(family)), s], send_sem.at[7])
        await_bytes(gathered.at[pl.ds(0, tiles // 2), s], send_sem.at[8])

    await_bytes(gamma_all.at[pl.ds(0, devices - 1)], recv_sem.at[4])
    gamma = jnp.sqrt(jnp.sum(gamma_all[...], axis=0))
    coef = beta * alpha / (alpha * alpha + gamma * gamma)
    solution_ref[...] = direction[...] * coef
    residual_ref[...] = rhs - image * coef
    await_bytes(gamma_all.at[pl.ds(0, devices - 1)], send_sem.at[9])


def shards(mat, signs, picks, rhs):
    devices = lax.axis_size("rows") * lax.axis_size("grp")
    rows, n = mat.shape
    tiles = n // TILE
    samp = picks.shape[0]
    planes = devices // tiles
    stages = planes.bit_length() - 1
    per = TILE // samp
    slots = (tiles * (tiles + 1) // 2 + tiles - 1) // tiles
    tables = planes // per * tiles
    if tables > 2 * tiles:
        tables = 1
    vmem = pl.BlockSpec(memory_space=pltpu.VMEM)
    f32, bf16, dma = jnp.float32, jnp.bfloat16, pltpu.SemaphoreType.DMA
    scratch = [
        ((rows, n), f32),
        ((tiles, rows, TILE), f32),
        ((tiles, rows, TILE), f32),
        ((1, TILE), jnp.int32),
        ((devices, 1, TILE), jnp.int32),
        ((tables, rows, TILE), bf16),
        ((tiles, rows, TILE), bf16),
        ((tiles, rows, TILE), bf16),
        ((planes, tiles * samp, TILE), f32),
        ((planes - 1, tiles * samp, TILE), f32),
        ((tiles, tiles * samp, TILE), f32),
        ((tiles, TILE + SUB, TILE), f32),
        ((tiles, TILE + SUB, TILE), f32),
        ((stages, slots + 1, TILE + SUB, TILE), f32),
        ((stages, slots + 1, TILE + SUB, TILE), f32),
        ((tiles, slots + 1, TILE, TILE), f32),
        ((n, TILE), f32),
        ((n, TILE), f32),
        ((n, n + TILE), bf16),
        ((n, n + TILE), bf16),
        ((rows, n), bf16),
        ((rows, n), bf16),
        ((n, TILE), f32),
        ((n, TILE), bf16),
        ((n, TILE), bf16),
        ((SUB, TILE), f32),
        ((1, TILE), f32),
        ((devices, 1, TILE), f32),
    ]
    return pl.pallas_call(
        step_kernel,
        out_shape=(
            jax.ShapeDtypeStruct((n, n), f32),
            jax.ShapeDtypeStruct((n, TILE), f32),
            jax.ShapeDtypeStruct((rows, TILE), f32),
        ),
        in_specs=[pl.BlockSpec(memory_space=pl.ANY)] + [vmem] * 3,
        out_specs=(vmem, vmem, vmem),
        scratch_shapes=[pltpu.VMEM(*entry) for entry in scratch] + [
            dma,
            dma((10,)),
            dma((5,)),
            dma((stages, tiles)),
            dma((tiles,)),
            dma((stages, slots + 1)),
            dma((slots + 1,)),
            dma((slots + 1,)),
        ],
        compiler_params=pltpu.CompilerParams(
            collective_id=0, has_side_effects=True, vmem_limit_bytes=(38 if tables > 1 else 56) * 1024 * 1024),
        name="sketch_solve",
    )(mat, signs.reshape(rows // TILE, TILE), picks.reshape(1, samp), rhs)


def solution(mesh):
    return jax.shard_map(
        shards,
        mesh=mesh,
        in_specs=(P(AXES, None), P(AXES), P(AXES), P(AXES, None)),
        out_specs=(P(), P(), P(AXES, None)),
        check_vma=False,
    )
```
